32 devices in a mesh: gx: 4 (over y, core), gy: 8 (over z, x).
Axes of the slice: x: 2, y: 2, z: 4, core: 2. Of those that a mesh axis runs over, the one named last changes fastest.
Arguments:
- columns: float32 [16384, 512], P(('gx', 'gy')), may hold values from -6 to 6
- col_basis: float32 [16384, 128], P(('gx', 'gy')), may hold values from -0.25 to 0.25
- row_basis: float32 [16384, 128], P(('gx', 'gy')), may hold values from -0.5 to 0.5
- order_perm: int32 [32, 512], P(('gx', 'gy')), may hold values from 0 to 511, each once within a row
- near_blocks: float32 [128, 5, 128, 128], P(('gx', 'gy')), may hold values from -0.25 to 0.25
- band_offsets: int32 [128, 5], P(('gx', 'gy')), may hold values from -4 to 4
- transfer: float32 [4, 2, 128, 128], replicated, may hold values from -0.375 to 0.375
- coupling: float32 [5, 128, 128], replicated, may hold values from -0.5 to 0.5
Outputs:
- product: float32 [16384, 512], P(('gx', 'gy'))
The draws below stay inside these ranges and needn't reach their ends.
Inputs may be any that keep to these rules, and one draw needn't show every extreme that they name: `order_perm`: each row is a permutation of the 512 rows of its leaf.
All inputs are finite; a program needn't handle non-finite values.
Results may differ from the reference program's by a relative error of at most 0.0001.
Values sent between devices are 32-bit elements; how exact they have to be, the bound alone decides.
No kernel may reach another device: no remote copies, remote signals or barrier semaphores. Data moves between devices by JAX's collectives and lax.ppermute only.
A program may use at most 64 MiB of HBM per device.

```python
import jax
import jax.numpy as jnp
from jax import lax

LEAF = 512
NRHS = 512
R = 128
BLK = 128
REACH = 4
NBAND = 5
LEVELS = 5
NBLK = 4
ORDER = 16384
DEVICES = 32


def place_ends(values, own_key, low, high):
    index_at = [jax.random.randint(jax.random.fold_in(own_key, axis), (), 0, length) for axis, length in enumerate(values.shape)]
    longest = values.shape.index(max(values.shape))
    neighbour = index_at[:longest] + [(index_at[longest] + 1) % values.shape[longest]] + index_at[longest + 1:]
    return values.at[tuple(index_at)].set(low).at[tuple(neighbour)].set(high)


def block_levels(key, dims, cuts, least, top_value):
    def one(dim, parts):
        steps = jax.random.uniform(jax.random.fold_in(jax.random.fold_in(key, 6), dim), (parts,), jnp.float32, least / len(cuts), top_value / len(cuts))
        return jnp.repeat(jnp.exp(steps), dims[dim] // parts).reshape((-1,) + (1,) * (len(dims) - dim - 1))

    level = one(*cuts[0])
    for cut in cuts[1:]:
        level = level * one(*cut)
    return level


def bell_draw(stream_key, shape, width, reach, split=(), held_as=jnp.bfloat16):
    entries = width * jax.random.normal(stream_key, shape, jnp.float32)
    if split:
        entries = entries * block_levels(stream_key, shape, split, -0.22, 0.18)
    return jnp.clip(entries, -reach, reach).astype(held_as)


def setup_inputs(seed: int = 0) -> dict:
    seeds = jax.random.split(jax.random.key(seed), 9)
    columns = bell_draw(seeds[0], (ORDER, NRHS), 1.0, 6.0, ((0, 32),), jnp.float32)
    col_basis = bell_draw(seeds[1], (ORDER, R), LEAF ** -0.5, 0.25, ((0, 32),), jnp.float32)
    row_basis = bell_draw(seeds[2], (ORDER, R), R ** -0.5, 0.5, ((0, 32),), jnp.float32)
    order_perm = jax.vmap(lambda own: jax.random.permutation(own, LEAF))(jax.random.split(seeds[3], DEVICES)).reshape((DEVICES, LEAF)).astype(jnp.int32)
    near_blocks = bell_draw(seeds[4], (DEVICES * NBLK, NBAND, BLK, BLK), (BLK * NBAND) ** -0.5, 0.25, ((0, 32),), jnp.float32)
    band_offsets = place_ends(jax.random.randint(seeds[5], (DEVICES * NBLK, NBAND), 0 - REACH, REACH + 1), jax.random.fold_in(seeds[5], 1), 0 - REACH, REACH).astype(jnp.int32)
    transfer = bell_draw(seeds[6], (LEVELS - 1, 2, R, R), (2 * R) ** -0.5, 0.375, (), jnp.float32)
    coupling = bell_draw(seeds[7], (LEVELS, R, R), R ** -0.5, 0.5, (), jnp.float32)
    return dict(columns=columns, col_basis=col_basis, row_basis=row_basis, order_perm=order_perm, near_blocks=near_blocks, band_offsets=band_offsets, transfer=transfer, coupling=coupling)


def near_field(padded_rows, blocks_here, offsets_here):
    rhs_cols = padded_rows.shape[1]
    column_blocks = padded_rows.reshape(-1, BLK, rhs_cols)
    block_index = jnp.arange(offsets_here.shape[0], dtype=jnp.int32)[:, None] + offsets_here + REACH
    taken = column_blocks[block_index]
    result = jnp.einsum("jbrc,jbcn->jrn", blocks_here, taken, precision=lax.Precision.HIGHEST)
    return result.reshape(-1, rhs_cols)


def reference(columns, col_basis, row_basis, order_perm, near_blocks, band_offsets, transfer, coupling):
    exact = lax.Precision.HIGHEST
    rhs_cols = columns.shape[1]
    leaves = columns.reshape(DEVICES, LEAF, rhs_cols)
    tree_cols = jnp.take_along_axis(leaves, order_perm[:, :, None], axis=1)
    skeleton = jnp.einsum("dlr,dln->drn", col_basis.reshape(DEVICES, LEAF, R), tree_cols, precision=exact)
    couples = []
    nodes = skeleton
    for level in range(LEVELS):
        pairs = nodes.reshape(-1, 2, R, rhs_cols)
        left_nodes = pairs[:, 0]
        right_nodes = pairs[:, 1]
        to_left = jnp.einsum("rk,pkn->prn", coupling[level], right_nodes, precision=exact)
        to_right = jnp.einsum("kr,pkn->prn", coupling[level], left_nodes, precision=exact)
        couples.append(jnp.stack([to_left, to_right], 1).reshape(-1, R, rhs_cols))
        if level < LEVELS - 1:
            nodes = jnp.einsum("kr,pkn->prn", transfer[level, 0], left_nodes, precision=exact) + jnp.einsum("kr,pkn->prn", transfer[level, 1], right_nodes, precision=exact)
    expand = couples[LEVELS - 1]
    for level in range(LEVELS - 2, -1, -1):
        down_left = jnp.einsum("rk,pkn->prn", transfer[level, 0], expand, precision=exact)
        down_right = jnp.einsum("rk,pkn->prn", transfer[level, 1], expand, precision=exact)
        expand = couples[level] + jnp.stack([down_left, down_right], 1).reshape(-1, R, rhs_cols)
    far = jnp.einsum("dlr,drn->dln", row_basis.reshape(DEVICES, LEAF, R), expand, precision=exact)
    margin = REACH * BLK
    padded = jnp.pad(tree_cols.reshape(ORDER, rhs_cols), ((margin, margin), (0, 0)))
    blocks_all = near_blocks.reshape(DEVICES, NBLK, NBAND, BLK, BLK)
    offsets_all = band_offsets.reshape(DEVICES, NBLK, NBAND)

    def one_leaf(inputs):
        leaf_index, blocks_here, offsets_here = inputs
        rows_here = lax.dynamic_slice_in_dim(padded, leaf_index * LEAF, LEAF + 2 * margin, 0)
        return near_field(rows_here, blocks_here, offsets_here)

    near = lax.map(one_leaf, (jnp.arange(DEVICES, dtype=jnp.int32), blocks_all, offsets_all))
    tree_out = near + far
    leaf_rows = jnp.arange(DEVICES, dtype=jnp.int32)[:, None]
    product = jnp.zeros_like(tree_out).at[leaf_rows, order_perm].set(tree_out)
    return product.reshape(ORDER, rhs_cols)
```

```python
import functools

import jax
import jax.numpy as jnp
from jax import lax
from jax.experimental import pallas as pl
from jax.experimental.pallas import tpu as pltpu
from jax.sharding import PartitionSpec as P

BLK = 128
REACH = 4
AXES = ("gx", "gy")
CHUNKS = (2, 2)
F32 = jnp.float32
BF16 = jnp.bfloat16


def split(x):
    high = x.astype(BF16)
    return high, (x - high.astype(F32)).astype(BF16)


def left_parts(x, axis):
    high, low = split(x)
    return jnp.concatenate([high, low, high], axis=axis)


def right_parts(x, axis):
    high, low = split(x)
    return jnp.concatenate([high, high, low], axis=axis)


def mm(a, b):
    return lax.dot_general(a, b, (((1,), (0,)), ((), ())), preferred_element_type=F32)


def mm_t(a, b):
    return lax.dot_general(a, b, (((1,), (1,)), ((), ())), preferred_element_type=F32)


def pick_rows(perm_row):
    length = perm_row.shape[1]
    column = jnp.transpose(jnp.broadcast_to(perm_row, (BLK, length)))
    parts = []
    for c in range(length // BLK):
        lanes = lax.broadcasted_iota(jnp.int32, (length, BLK), 1) + c * BLK
        parts.append(jnp.where(column == lanes, 1.0, 0.0).astype(BF16))
    return jnp.concatenate(parts, axis=1)


def place_rows(perm_row):
    length = perm_row.shape[1]
    rows = lax.broadcasted_iota(jnp.int32, (length, length), 0)
    return jnp.where(rows == perm_row, 1.0, 0.0).astype(BF16)


def first_kernel(perm_ref, x_ref, basis_ref, skel_ref, *chunk_refs):
    width = x_ref.shape[1]
    high, low = split(x_ref[...])
    both = mm(pick_rows(perm_ref[...]), jnp.concatenate([high, low], axis=1))
    tree = both[:, :width] + both[:, width:]
    start = 0
    for ref in chunk_refs:
        ref[...] = tree[start : start + ref.shape[0]]
        start += ref.shape[0]
    basis = left_parts(jnp.transpose(basis_ref[...]), 1)
    skel = mm(basis, right_parts(tree, 0))
    skel_ref[...] = jnp.transpose(skel)


def weights_kernel(transfer_ref, coupling_ref, left_ref, right_ref, down_ref):
    levels = coupling_ref.shape[0]
    for m in range(levels):
        couple = coupling_ref[m]
        t = min(m, levels - 2)
        left = jnp.concatenate([transfer_ref[t, 0], couple], axis=1)
        right = jnp.concatenate([transfer_ref[t, 1], jnp.transpose(couple)], axis=1)
        left_ref[m] = right_parts(left, 0)
        right_ref[m] = right_parts(right, 0)
        if m < levels - 1:
            down = jnp.concatenate(
                [jnp.transpose(transfer_ref[m, 0]), jnp.transpose(transfer_ref[m, 1])], axis=1
            )
            down_ref[m] = right_parts(down, 0)


def tree_kernel(width, s_ref, left_ref, right_ref, down_ref, e_ref):
    levels = left_ref.shape[0]
    rank = s_ref.shape[1]
    nodes = s_ref[...]
    couples = []
    for m in range(levels):
        pairs = nodes.reshape(-1, 2, width, rank)
        lefts = left_parts(pairs[:, 0].reshape(-1, rank), 1)
        rights = left_parts(pairs[:, 1].reshape(-1, rank), 1)
        from_left = mm(lefts, left_ref[m])
        from_right = mm(rights, right_ref[m])
        nodes = from_left[:, :rank] + from_right[:, :rank]
        couples.append((from_right[:, rank:], from_left[:, rank:]))

    def joined(a, b):
        a = a.reshape(-1, 1, width, rank)
        b = b.reshape(-1, 1, width, rank)
        return jnp.concatenate([a, b], axis=1).reshape(-1, rank)

    expand = joined(*couples[levels - 1])
    for m in range(levels - 2, -1, -1):
        down = mm(left_parts(expand, 1), down_ref[m])
        expand = joined(couples[m][0] + down[:, :rank], couples[m][1] + down[:, rank:])
    e_ref[...] = expand


def tree_plain(s, transfer, coupling, width):
    exact = lax.Precision.HIGHEST
    levels, rank = coupling.shape[:2]
    nodes = s
    couples = []
    for m in range(levels):
        pairs = nodes.reshape(-1, 2, width, rank)
        left, right = pairs[:, 0], pairs[:, 1]
        to_left = jnp.einsum("pnk,rk->pnr", right, coupling[m], precision=exact)
        to_right = jnp.einsum("pnk,kr->pnr", left, coupling[m], precision=exact)
        couples.append(jnp.stack([to_left, to_right], 1))
        if m < levels - 1:
            nodes = jnp.einsum("pnk,kr->pnr", left, transfer[m, 0], precision=exact)
            nodes = nodes + jnp.einsum("pnk,kr->pnr", right, transfer[m, 1], precision=exact)
    expand = couples[levels - 1]
    for m in range(levels - 2, -1, -1):
        parent = expand.reshape(-1, width, rank)
        down = jnp.einsum("pnk,srk->psnr", parent, transfer[m], precision=exact)
        expand = couples[m] + down
    return expand.reshape(-1, rank)


def last_kernel(n_chunks, offsets_ref, perm_ref, blocks_ref, basis_ref, expand_ref, *rest):
    own_refs = rest[:n_chunks]
    sib_refs = rest[n_chunks : 2 * n_chunks]
    fwd_refs = rest[2 * n_chunks : 3 * n_chunks]
    out_ref, high_ref, low_ref, acc_ref = rest[3 * n_chunks :]
    n_rows, n_band = offsets_ref.shape
    slot = 0
    for refs in (own_refs, sib_refs, fwd_refs):
        for ref in refs:
            for c in range(ref.shape[0] // BLK):
                high, low = split(ref[c * BLK : (c + 1) * BLK, :])
                high_ref[slot] = high
                low_ref[slot] = low
                slot += 1
    odd = lax.rem(lax.axis_index("gy"), 2)
    left_base = jnp.where(odd == 1, n_rows, 2 * n_rows)
    right_base = jnp.where(odd == 1, 2 * n_rows, n_rows)
    expand = right_parts(expand_ref[...], 1)
    for i in range(n_rows):
        rows = slice(i * BLK, (i + 1) * BLK)
        total = mm_t(left_parts(basis_ref[rows, :], 1), expand)
        for j in range(n_band):
            t = offsets_ref[i, j] + i
            at = jnp.where(
                t < 0, left_base + t + n_rows, jnp.where(t < n_rows, t, right_base + t - n_rows)
            )
            high = high_ref[at]
            low = low_ref[at]
            total += mm(
                left_parts(blocks_ref[i, j], 1), jnp.concatenate([high, high, low], axis=0)
            )
        acc_ref[rows, :] = total
    high, low = split(acc_ref[...])
    width = out_ref.shape[1]
    both = mm(place_rows(perm_ref[...]), jnp.concatenate([high, low], axis=1))
    out_ref[...] = both[:, :width] + both[:, width:]


def vmem(n):
    return [pl.BlockSpec(memory_space=pltpu.VMEM)] * n


def per_device(
    columns, col_basis, row_basis, order_perm, near_blocks, band_offsets, transfer, coupling
):
    across, along = lax.axis_size("gx"), lax.axis_size("gy")
    devices = across * along
    leaf, width = columns.shape
    rank = col_basis.shape[1]
    levels = coupling.shape[0]
    n_rows = leaf // BLK
    share = width // devices
    sibling = [(d, d ^ 1) for d in range(devices)]
    forward = []
    for d in range(devices):
        held = d ^ 1
        to = held + 1 if held % 2 else held - 1
        if 0 <= to < devices:
            forward.append((d, to))

    chunk_shapes = [jax.ShapeDtypeStruct((c * BLK, width), F32) for c in CHUNKS]
    first = pl.pallas_call(
        first_kernel,
        out_shape=[jax.ShapeDtypeStruct((width, rank), F32)] + chunk_shapes,
        in_specs=vmem(3),
        out_specs=vmem(1 + len(CHUNKS)),
        name="first",
    )(order_perm, columns, col_basis)
    skel, own = first[0], first[1:]

    sib = [lax.ppermute(c, AXES, sibling) for c in own]
    fwd = [lax.ppermute(c, AXES, forward) for c in sib]

    gathered = lax.all_to_all(skel.reshape(devices, share, rank), AXES, 0, 0)
    gathered = gathered.reshape(width, rank)
    if share % 8 == 0:
        weights = pl.pallas_call(
            weights_kernel,
            out_shape=[
                jax.ShapeDtypeStruct((levels, 3 * rank, 2 * rank), BF16),
                jax.ShapeDtypeStruct((levels, 3 * rank, 2 * rank), BF16),
                jax.ShapeDtypeStruct((levels - 1, 3 * rank, 2 * rank), BF16),
            ],
            in_specs=vmem(2),
            out_specs=vmem(3),
            name="weights",
        )(transfer, coupling)
        expand = pl.pallas_call(
            functools.partial(tree_kernel, share),
            out_shape=jax.ShapeDtypeStruct((width, rank), F32),
            in_specs=vmem(4),
            out_specs=vmem(1)[0],
            name="tree",
        )(gathered, *weights)
    else:
        expand = tree_plain(gathered, transfer, coupling, share)
    expand = lax.all_to_all(expand.reshape(devices, share, rank), AXES, 0, 0)
    expand = expand.reshape(width, rank)

    return pl.pallas_call(
        functools.partial(last_kernel, len(CHUNKS)),
        out_shape=jax.ShapeDtypeStruct((leaf, width), F32),
        in_specs=[pl.BlockSpec(memory_space=pltpu.SMEM)] + vmem(4 + 3 * len(CHUNKS)),
        out_specs=vmem(1)[0],
        scratch_shapes=[
            pltpu.VMEM((3 * leaf // BLK, BLK, width), BF16),
            pltpu.VMEM((3 * leaf // BLK, BLK, width), BF16),
            pltpu.VMEM((leaf, width), F32),
        ],
        name="last",
    )(band_offsets, order_perm, near_blocks, row_basis, expand, *own, *sib, *fwd)


def solution(mesh):
    placed = (
        P(("gx", "gy"), None),
        P(("gx", "gy"), None),
        P(("gx", "gy"), None),
        P(("gx", "gy"), None),
        P(("gx", "gy"), None, None, None),
        P(("gx", "gy"), None),
        P(),
        P(),
    )
    return jax.shard_map(
        per_device, mesh=mesh, in_specs=placed, out_specs=P(("gx", "gy"), None), check_vma=False
    )
```

```python
import functools

import jax
import jax.numpy as jnp
from jax import lax
from jax.experimental import pallas as pl
from jax.experimental.pallas import tpu as pltpu
from jax.sharding import PartitionSpec as P


BLK = 128
AXES = ("gx", "gy")
CHUNKS = ((1, False), (1, False), (2, False))
LATE = ('f2',)
OUT_COPIES = 8
PIECES = 4
TREE_MIB = 10
LAST_MIB = 14
F32 = jnp.float32
BF16 = jnp.bfloat16


def split(x):
    high = x.astype(BF16)
    return high, (x - high.astype(F32)).astype(BF16)


def left_parts(x, axis):
    high, low = split(x)
    return jnp.concatenate([high, low, high], axis=axis)


def right_parts(x, axis):
    high, low = split(x)
    return jnp.concatenate([high, high, low], axis=axis)


def mm(a, b):
    return lax.dot_general(a, b, (((1,), (0,)), ((), ())), preferred_element_type=F32)


def mm_t(a, b):
    return lax.dot_general(a, b, (((1,), (1,)), ((), ())), preferred_element_type=F32)


def pick_rows(perm_row):
    length = perm_row.shape[1]
    column = jnp.transpose(jnp.broadcast_to(perm_row, (BLK, length)))
    parts = []
    for c in range(length // BLK):
        lanes = lax.broadcasted_iota(jnp.int32, (length, BLK), 1) + c * BLK
        parts.append(jnp.where(column == lanes, 1.0, 0.0).astype(BF16))
    return jnp.concatenate(parts, axis=1)


def place_rows(perm_row):
    length = perm_row.shape[1]
    rows = lax.broadcasted_iota(jnp.int32, (length, length), 0)
    return jnp.where(rows == perm_row, 1.0, 0.0).astype(BF16)


def first_kernel(perm_ref, x_ref, basis_ref, skel_ref, *chunk_refs):
    high, low = split(x_ref[...])
    pick = pick_rows(perm_ref[...])
    tree = mm(jnp.concatenate([pick, pick], axis=1), jnp.concatenate([high, low], axis=0))
    start = 0
    for ref in chunk_refs:
        ref[...] = tree[start : start + ref.shape[0]]
        start += ref.shape[0]
    basis = left_parts(jnp.transpose(basis_ref[...]), 1)
    skel = mm(basis, right_parts(tree, 0))
    skel_ref[...] = jnp.transpose(skel)


class Stage:
    def __init__(self, refs, n_smem, n_in, n_out):
        self.smem, refs = refs[:n_smem], refs[n_smem:]
        self.source, refs = refs[:n_in], refs[n_in:]
        self.target, refs = refs[:n_out], refs[n_out:]
        self.inside, refs = refs[:n_in], refs[n_in:]
        self.outside, refs = refs[:n_out], refs[n_out:]
        *self.scratch, self.in_sems, self.out_sems = refs
        self.loads = [
            pltpu.make_async_copy(a, b, self.in_sems.at[n])
            for n, (a, b) in enumerate(zip(self.source, self.inside))
        ]
        for load in self.loads:
            load.start()
        self.pending = set(range(n_in))
        self.stores = []

    def get(self, n):
        if n in self.pending:
            self.pending.remove(n)
            self.loads[n].wait()
        return self.inside[n]

    def rows(self, numbers):
        return jnp.concatenate([self.get(n)[...] for n in numbers], axis=0)

    def put(self, n, value, start=None):
        at = () if start is None else (pl.ds(start, value.shape[0]),)
        held = self.outside[n].at[at] if at else self.outside[n]
        held[...] = value
        store = pltpu.make_async_copy(
            held,
            self.target[n].at[at] if at else self.target[n],
            self.out_sems.at[len(self.stores)],
        )
        store.start()
        self.stores.append(store)

    def finish(self):
        assert not self.pending
        for store in self.stores:
            store.wait()


def staged(body, inputs, out_shapes, smem=(), scratch=(), mib=None):
    sizes = (len(smem), len(inputs), len(out_shapes))

    def kernel(*refs):
        stage = Stage(refs, *sizes)
        body(stage)
        stage.finish()

    return pl.pallas_call(
        kernel,
        out_shape=[jax.ShapeDtypeStruct(shape, dtype) for shape, dtype in out_shapes],
        in_specs=[pl.BlockSpec(memory_space=pltpu.SMEM)] * len(smem) + hbm(len(inputs)),
        out_specs=hbm(len(out_shapes)),
        scratch_shapes=[pltpu.VMEM(a.shape, a.dtype) for a in inputs]
        + [pltpu.VMEM(shape, dtype) for shape, dtype in out_shapes]
        + list(scratch)
        + [pltpu.SemaphoreType.DMA((len(inputs),)), pltpu.SemaphoreType.DMA((OUT_COPIES,))],
        compiler_params=None if mib is None else limit(mib),
    )(*smem, *inputs)


def prep_kernel(near_slots, late_slots, stage):
    (offsets_ref,), (dense_ref,) = stage.smem, stage.scratch
    n_rows, n_band = offsets_ref.shape
    odd = lax.rem(lax.axis_index("gy"), 2)
    left_base = jnp.where(odd == 1, n_rows, 2 * n_rows)
    right_base = jnp.where(odd == 1, 2 * n_rows, n_rows)
    dense_ref[...] = jnp.zeros_like(dense_ref)
    blocks_ref = stage.get(0)
    for i in range(n_rows):
        rows = slice(i * BLK, (i + 1) * BLK)
        for j in range(n_band):
            t = offsets_ref[i, j] + i
            at = jnp.where(
                t < 0, left_base + t + n_rows, jnp.where(t < n_rows, t, right_base + t - n_rows)
            )
            dense_ref[at, rows, :] += blocks_ref[i, j]

    def joined(slots):
        return split(jnp.concatenate([dense_ref[at] for at in slots], axis=1))

    high, low = joined(near_slots)
    stage.put(1, jnp.stack([high, low]))
    high, low = joined(range(n_rows))
    stage.put(
        0,
        mm(
            jnp.concatenate([high, low, high], axis=1),
            right_parts(stage.rows(range(3, len(stage.inside))), 0),
        ),
    )
    place = place_rows(stage.get(1)[...])
    high, low = joined(late_slots)
    stage.put(2, jnp.stack([mm(place, high).astype(BF16), mm(place, low).astype(BF16)]))
    high, low = split(stage.get(2)[...])
    stage.put(3, jnp.stack([mm(place, high).astype(BF16), mm(place, low).astype(BF16)]))


def left_pair(ref, *at):
    high, low = ref[(*at, 0)], ref[(*at, 1)]
    return jnp.concatenate([high, low, high], axis=1)


def tree_kernel(width, stage):
    coupling_ref, transfer_ref = stage.get(1), stage.get(2)
    levels, rank = coupling_ref.shape[:2]
    down_c = [right_parts(coupling_ref[m], 1) for m in range(levels)]
    up_c = [right_parts(coupling_ref[m], 0) for m in range(levels)]
    up_t = [[right_parts(transfer_ref[m, h], 0) for h in range(2)] for m in range(levels - 1)]
    down_t = [[right_parts(transfer_ref[m, h], 1) for h in range(2)] for m in range(levels - 1)]
    nodes = stage.get(0)[...]
    couples = []
    for m in range(levels):
        pairs = nodes.reshape(-1, 2, width, rank)
        lefts = left_parts(pairs[:, 0].reshape(-1, rank), 1)
        rights = left_parts(pairs[:, 1].reshape(-1, rank), 1)
        couples.append((mm_t(rights, down_c[m]), mm(lefts, up_c[m])))
        if m < levels - 1:
            nodes = mm(lefts, up_t[m][0]) + mm(rights, up_t[m][1])

    def joined(a, b):
        a = a.reshape(-1, 1, width, rank)
        b = b.reshape(-1, 1, width, rank)
        return jnp.concatenate([a, b], axis=1).reshape(-1, rank)

    expand = joined(*couples[levels - 1])
    for m in range(levels - 2, -1, -1):
        parents = left_parts(expand, 1)
        left = mm_t(parents, down_t[m][0])
        right = mm_t(parents, down_t[m][1])
        expand = joined(couples[m][0] + left, couples[m][1] + right)
    stage.put(0, expand)


def tree_plain(s, transfer, coupling, width):
    exact = lax.Precision.HIGHEST
    levels, rank = coupling.shape[:2]
    nodes = s
    couples = []
    for m in range(levels):
        pairs = nodes.reshape(-1, 2, width, rank)
        left, right = pairs[:, 0], pairs[:, 1]
        to_left = jnp.einsum("pnk,rk->pnr", right, coupling[m], precision=exact)
        to_right = jnp.einsum("pnk,kr->pnr", left, coupling[m], precision=exact)
        couples.append(jnp.stack([to_left, to_right], 1))
        if m < levels - 1:
            nodes = jnp.einsum("pnk,kr->pnr", left, transfer[m, 0], precision=exact)
            nodes = nodes + jnp.einsum("pnk,kr->pnr", right, transfer[m, 1], precision=exact)
    expand = couples[levels - 1]
    for m in range(levels - 2, -1, -1):
        parent = expand.reshape(-1, width, rank)
        down = jnp.einsum("pnk,srk->psnr", parent, transfer[m], precision=exact)
        expand = couples[m] + down
    return expand.reshape(-1, rank)


def near_kernel(stage):
    total = mm(left_pair(stage.get(2)), right_parts(stage.rows(range(3, len(stage.inside))), 0))
    high, low = split(stage.get(1)[...] + total)
    both = jnp.concatenate([high, low], axis=0)
    place = place_rows(stage.get(0)[...])
    place = jnp.concatenate([place, place], axis=1)
    step = place.shape[0] // PIECES
    for start in range(0, place.shape[0], step):
        stage.put(0, mm(place[start : start + step], both), start)


def last_kernel(stage):
    expand = right_parts(stage.get(0)[...], 1)
    far = mm_t(left_pair(stage.get(1)), expand)
    left = left_pair(stage.get(2))
    rows = right_parts(stage.rows(range(4, len(stage.inside))), 0)
    sum_ref = stage.get(3)
    step = left.shape[0] // PIECES
    for start in range(0, left.shape[0], step):
        at = slice(start, start + step)
        stage.put(0, sum_ref[at, :] + far[at] + mm(left[at], rows), start)


def limit(mib):
    return pltpu.CompilerParams(vmem_limit_bytes=mib << 20)


def hbm(n):
    return [pl.BlockSpec(memory_space=pltpu.HBM)] * n


def vmem(n):
    return [pl.BlockSpec(memory_space=pltpu.VMEM)] * n


def body(
    columns, col_basis, row_basis, order_perm, near_blocks, band_offsets, transfer, coupling
):
    across, along = lax.axis_size("gx"), lax.axis_size("gy")
    devices = across * along
    leaf, width = columns.shape
    n_rows = leaf // BLK
    rank = col_basis.shape[1]
    share = width // devices
    sibling = [(d, d ^ 1) for d in range(devices)]
    diagonal = [(d, d + 1 if d % 2 else d - 1) for d in range(1, devices - 1)]
    forward = []
    for d in range(devices):
        to = d - 2 if d % 2 else d + 2
        if 0 <= to < devices:
            forward.append((d, to))

    rows = [c * leaf // sum(n for n, _ in CHUNKS) for c, _ in CHUNKS]
    chunk_shapes = [jax.ShapeDtypeStruct((n, width), F32) for n in rows]
    n_chunks = len(CHUNKS)
    first = pl.pallas_call(
        first_kernel,
        out_shape=[jax.ShapeDtypeStruct((width, rank), F32)] + chunk_shapes,
        in_specs=vmem(3),
        out_specs=vmem(1 + n_chunks),
        name="first",
    )(order_perm, columns, col_basis)
    skel, own = first[0], list(first[1:])

    pieces = {}
    start = 0
    for c, (blocks, direct) in enumerate(CHUNKS):
        sib = lax.ppermute(own[c], AXES, sibling)
        if direct:
            fwd = lax.ppermute(own[c], AXES, diagonal)
        else:
            fwd = lax.ppermute(sib, AXES, forward)
        blocks = rows[c] // BLK
        pieces[f"s{c}"] = (sib, range(n_rows + start, n_rows + start + blocks))
        pieces[f"f{c}"] = (fwd, range(2 * n_rows + start, 2 * n_rows + start + blocks))
        start += blocks
    early = [pieces[p] for p in pieces if p not in LATE]
    late = [pieces[p] for p in LATE]
    near_slots = [at for _, slots in early for at in slots]
    late_slots = [at for _, slots in late for at in slots]

    own_sum, near, left, far = staged(
        functools.partial(prep_kernel, near_slots, late_slots),
        [near_blocks, order_perm, row_basis] + own,
        [
            ((leaf, width), F32),
            ((2, leaf, len(near_slots) * BLK), BF16),
            ((2, leaf, len(late_slots) * BLK), BF16),
            ((2, leaf, rank), BF16),
        ],
        smem=[band_offsets],
        scratch=[pltpu.VMEM((3 * n_rows, leaf, BLK), F32)],
    )

    gathered = lax.all_to_all(skel.reshape(devices, share, rank), AXES, 0, 0)
    gathered = gathered.reshape(width, rank)
    if share % 8 == 0:
        (expand,) = staged(
            functools.partial(tree_kernel, share),
            [gathered, coupling, transfer],
            [((width, rank), F32)],
            mib=TREE_MIB,
        )
    else:
        expand = tree_plain(gathered, transfer, coupling, share)
    expand = lax.all_to_all(expand.reshape(devices, share, rank), AXES, 0, 0)
    expand = expand.reshape(width, rank)

    (total,) = staged(
        near_kernel,
        [order_perm, own_sum, near] + [rows for rows, _ in early],
        [((leaf, width), F32)],
    )
    (product,) = staged(
        last_kernel,
        [expand, far, left, total] + [rows for rows, _ in late],
        [((leaf, width), F32)],
        mib=LAST_MIB,
    )
    return product


def solution(mesh):
    split_rows = P(("gx", "gy"), None)
    placed = (split_rows,) * 4 + (P(("gx", "gy"), None, None, None), split_rows, P(), P())
    return jax.shard_map(body, mesh=mesh, in_specs=placed, out_specs=split_rows, check_vma=False)
```

```python
import functools

import jax
import jax.numpy as jnp
from jax import lax
from jax.experimental import pallas as pl
from jax.experimental.pallas import tpu as pltpu
from jax.sharding import PartitionSpec as P


BLK = 128
AXES = ("gx", "gy")
CHUNKS = ((1, False), (1, False), (1, False), (1, True))
LATE = ('f3',)
OUT_COPIES = 8
PIECES = 4
TREE_MIB = 10
LAST_MIB = 14
F32 = jnp.float32
BF16 = jnp.bfloat16


def split(x):
    high = x.astype(BF16)
    return high, (x - high.astype(F32)).astype(BF16)


def left_parts(x, axis):
    high, low = split(x)
    return jnp.concatenate([high, low, high], axis=axis)


def right_parts(x, axis):
    high, low = split(x)
    return jnp.concatenate([high, high, low], axis=axis)


def mm(a, b):
    return lax.dot_general(a, b, (((1,), (0,)), ((), ())), preferred_element_type=F32)


def mm_t(a, b):
    return lax.dot_general(a, b, (((1,), (1,)), ((), ())), preferred_element_type=F32)


def pick_rows(perm_row):
    length = perm_row.shape[1]
    column = jnp.transpose(jnp.broadcast_to(perm_row, (BLK, length)))
    parts = []
    for c in range(length // BLK):
        lanes = lax.broadcasted_iota(jnp.int32, (length, BLK), 1) + c * BLK
        parts.append(jnp.where(column == lanes, 1.0, 0.0).astype(BF16))
    return jnp.concatenate(parts, axis=1)


def place_rows(perm_row):
    length = perm_row.shape[1]
    rows = lax.broadcasted_iota(jnp.int32, (length, length), 0)
    return jnp.where(rows == perm_row, 1.0, 0.0).astype(BF16)


def first_kernel(perm_ref, x_ref, basis_ref, skel_ref, *chunk_refs):
    high, low = split(x_ref[...])
    pick = pick_rows(perm_ref[...])
    tree = mm(jnp.concatenate([pick, pick], axis=1), jnp.concatenate([high, low], axis=0))
    start = 0
    for ref in chunk_refs:
        ref[...] = tree[start : start + ref.shape[0]]
        start += ref.shape[0]
    basis = left_parts(jnp.transpose(basis_ref[...]), 1)
    skel = mm(basis, right_parts(tree, 0))
    skel_ref[...] = jnp.transpose(skel)


class Stage:
    def __init__(self, refs, n_smem, n_in, n_out):
        self.smem, refs = refs[:n_smem], refs[n_smem:]
        self.source, refs = refs[:n_in], refs[n_in:]
        self.target, refs = refs[:n_out], refs[n_out:]
        self.inside, refs = refs[:n_in], refs[n_in:]
        self.outside, refs = refs[:n_out], refs[n_out:]
        *self.scratch, self.in_sems, self.out_sems = refs
        self.loads = [
            pltpu.make_async_copy(a, b, self.in_sems.at[n])
            for n, (a, b) in enumerate(zip(self.source, self.inside))
        ]
        for load in self.loads:
            load.start()
        self.pending = set(range(n_in))
        self.stores = []

    def get(self, n):
        if n in self.pending:
            self.pending.remove(n)
            self.loads[n].wait()
        return self.inside[n]

    def rows(self, numbers):
        return jnp.concatenate([self.get(n)[...] for n in numbers], axis=0)

    def put(self, n, value, start=None):
        at = () if start is None else (pl.ds(start, value.shape[0]),)
        held = self.outside[n].at[at] if at else self.outside[n]
        held[...] = value
        store = pltpu.make_async_copy(
            held,
            self.target[n].at[at] if at else self.target[n],
            self.out_sems.at[len(self.stores)],
        )
        store.start()
        self.stores.append(store)

    def finish(self):
        assert not self.pending
        for store in self.stores:
            store.wait()


def staged(body, inputs, out_shapes, smem=(), scratch=(), mib=None):
    sizes = (len(smem), len(inputs), len(out_shapes))

    def kernel(*refs):
        stage = Stage(refs, *sizes)
        body(stage)
        stage.finish()

    return pl.pallas_call(
        kernel,
        out_shape=[jax.ShapeDtypeStruct(shape, dtype) for shape, dtype in out_shapes],
        in_specs=[pl.BlockSpec(memory_space=pltpu.SMEM)] * len(smem) + hbm(len(inputs)),
        out_specs=hbm(len(out_shapes)),
        scratch_shapes=[pltpu.VMEM(a.shape, a.dtype) for a in inputs]
        + [pltpu.VMEM(shape, dtype) for shape, dtype in out_shapes]
        + list(scratch)
        + [pltpu.SemaphoreType.DMA((len(inputs),)), pltpu.SemaphoreType.DMA((OUT_COPIES,))],
        compiler_params=None if mib is None else limit(mib),
    )(*smem, *inputs)


def slot_of(offset, row, n_rows):
    odd = lax.rem(lax.axis_index("gy"), 2)
    left_base = jnp.where(odd == 1, n_rows, 2 * n_rows)
    right_base = jnp.where(odd == 1, 2 * n_rows, n_rows)
    t = offset + row
    return jnp.where(
        t < 0, left_base + t + n_rows, jnp.where(t < n_rows, t, right_base + t - n_rows)
    )


def left_pair(ref, *at):
    high, low = ref[(*at, 0)], ref[(*at, 1)]
    return jnp.concatenate([high, low, high], axis=1)


def tree_kernel(width, stage):
    coupling_ref, transfer_ref = stage.get(1), stage.get(2)
    levels, rank = coupling_ref.shape[:2]
    last = levels - 1

    def paired(m, side):
        couple = coupling_ref[m]
        couple = jnp.transpose(couple) if side else couple
        parts = [couple] if m == last else [couple, transfer_ref[m, side]]
        return right_parts(jnp.concatenate(parts, axis=1), 0)

    ups = [[paired(m, side) for side in range(2)] for m in range(levels)]
    downs = [
        right_parts(jnp.concatenate([transfer_ref[m, 0], transfer_ref[m, 1]], axis=0), 1)
        for m in range(last)
    ]
    nodes = stage.get(0)[...]
    couples = []
    for m in range(levels):
        pairs = nodes.reshape(-1, 2, width, rank)
        lefts = left_parts(pairs[:, 0].reshape(-1, rank), 1)
        rights = left_parts(pairs[:, 1].reshape(-1, rank), 1)
        from_left, from_right = mm(lefts, ups[m][0]), mm(rights, ups[m][1])
        couples.append((from_right[:, :rank], from_left[:, :rank]))
        if m < last:
            nodes = from_left[:, rank:] + from_right[:, rank:]

    def joined(a, b):
        a = a.reshape(-1, 1, width, rank)
        b = b.reshape(-1, 1, width, rank)
        return jnp.concatenate([a, b], axis=1).reshape(-1, rank)

    expand = joined(*couples[levels - 1])
    for m in range(levels - 2, -1, -1):
        parents = left_parts(expand, 1)
        down = mm_t(parents, downs[m])
        expand = joined(couples[m][0] + down[:, :rank], couples[m][1] + down[:, rank:])
    stage.put(0, expand)


def tree_plain(s, transfer, coupling, width):
    exact = lax.Precision.HIGHEST
    levels, rank = coupling.shape[:2]
    nodes = s
    couples = []
    for m in range(levels):
        pairs = nodes.reshape(-1, 2, width, rank)
        left, right = pairs[:, 0], pairs[:, 1]
        to_left = jnp.einsum("pnk,rk->pnr", right, coupling[m], precision=exact)
        to_right = jnp.einsum("pnk,kr->pnr", left, coupling[m], precision=exact)
        couples.append(jnp.stack([to_left, to_right], 1))
        if m < levels - 1:
            nodes = jnp.einsum("pnk,kr->pnr", left, transfer[m, 0], precision=exact)
            nodes = nodes + jnp.einsum("pnk,kr->pnr", right, transfer[m, 1], precision=exact)
    expand = couples[levels - 1]
    for m in range(levels - 2, -1, -1):
        parent = expand.reshape(-1, width, rank)
        down = jnp.einsum("pnk,srk->psnr", parent, transfer[m], precision=exact)
        expand = couples[m] + down
    return expand.reshape(-1, rank)


def near_kernel(slots, late_slots, stage):
    (offsets_ref,), (high_ref, low_ref, sum_ref, dense_ref) = stage.smem, stage.scratch
    n_rows, n_band = offsets_ref.shape
    n_late = len(late_slots)
    place = place_rows(stage.get(0)[...])
    for late in late_slots:
        high_ref[late] = jnp.zeros(high_ref.shape[1:], BF16)
        low_ref[late] = jnp.zeros(low_ref.shape[1:], BF16)
    dense_ref[...] = jnp.zeros_like(dense_ref)
    blocks_ref = stage.get(1)
    where = {}
    for i in range(n_rows):
        rows = slice(i * BLK, (i + 1) * BLK)
        for j in range(n_band):
            where[i, j] = slot_of(offsets_ref[i, j], i, n_rows)
            at = n_late
            for k, late in enumerate(late_slots):
                at = jnp.where(where[i, j] == late, k, at)
            dense_ref[at, rows, :] += blocks_ref[i, j]
    dense = jnp.concatenate([dense_ref[k] for k in range(n_late)], axis=1)
    parts = [*split(dense), *split(stage.get(2)[...])]
    moved = mm(place, jnp.concatenate(parts, axis=1)).astype(BF16)
    tail, rank = parts[0].shape[1], parts[2].shape[1]
    stage.put(1, jnp.stack([moved[:, :tail], moved[:, tail : 2 * tail]]))
    stage.put(2, jnp.stack([moved[:, 2 * tail : 2 * tail + rank], moved[:, 2 * tail + rank :]]))
    for n, group in enumerate(slots):
        piece = stage.get(n + 3)
        for k, at in enumerate(group):
            high_ref[at], low_ref[at] = split(piece[k * BLK : (k + 1) * BLK, :])
    for i in range(n_rows):
        left, right = [], []
        for j in range(n_band):
            left.append(left_parts(blocks_ref[i, j], 1))
            high, low = high_ref[where[i, j]], low_ref[where[i, j]]
            right += [high, high, low]
        sum_ref[i * BLK : (i + 1) * BLK, :] = mm(
            jnp.concatenate(left, axis=1), jnp.concatenate(right, axis=0)
        )
    both = jnp.concatenate(split(sum_ref[...]), axis=0)
    stage.put(0, mm(jnp.concatenate([place, place], axis=1), both))


def last_kernel(stage):
    expand = right_parts(stage.get(0)[...], 1)
    far = mm_t(left_pair(stage.get(1)), expand)
    left = left_pair(stage.get(2))
    rows = right_parts(stage.rows(range(4, len(stage.inside))), 0)
    sum_ref = stage.get(3)
    step = left.shape[0] // PIECES
    for start in range(0, left.shape[0], step):
        at = slice(start, start + step)
        stage.put(0, sum_ref[at, :] + far[at] + mm(left[at], rows), start)


def limit(mib):
    return pltpu.CompilerParams(vmem_limit_bytes=mib << 20)


def in_hbm(x):
    return pltpu.with_memory_space_constraint(x, pltpu.HBM)


def hbm(n):
    return [pl.BlockSpec(memory_space=pltpu.HBM)] * n


def vmem(n):
    return [pl.BlockSpec(memory_space=pltpu.VMEM)] * n


def body(
    columns, col_basis, row_basis, order_perm, near_blocks, band_offsets, transfer, coupling
):
    across, along = lax.axis_size("gx"), lax.axis_size("gy")
    devices = across * along
    leaf, width = columns.shape
    n_rows = leaf // BLK
    rank = col_basis.shape[1]
    share = width // devices
    sibling = [(d, d ^ 1) for d in range(devices)]
    forward = []
    for d in range(devices):
        to = d - 2 if d % 2 else d + 2
        if 0 <= to < devices:
            forward.append((d, to))
    backward = [(to, d) for d, to in forward]

    rows = [c * leaf // sum(n for n, _ in CHUNKS) for c, _ in CHUNKS]
    chunk_shapes = [jax.ShapeDtypeStruct((n, width), F32) for n in rows]
    n_chunks = len(CHUNKS)
    first = pl.pallas_call(
        first_kernel,
        out_shape=[jax.ShapeDtypeStruct((width, rank), F32)] + chunk_shapes,
        in_specs=vmem(3),
        out_specs=vmem(1 + n_chunks),
        name="first",
    )(order_perm, columns, col_basis)
    skel, own = first[0], list(first[1:])

    pieces = {}
    start = 0
    for c, (blocks, direct) in enumerate(CHUNKS):
        sib = lax.ppermute(own[c], AXES, sibling)
        if direct:
            fwd = lax.ppermute(own[c], AXES, backward)
            fwd = lax.ppermute(fwd, AXES, sibling)
        else:
            fwd = lax.ppermute(sib, AXES, forward)
        blocks = rows[c] // BLK
        pieces[f"o{c}"] = (own[c], range(start, start + blocks))
        pieces[f"s{c}"] = (sib, range(n_rows + start, n_rows + start + blocks))
        pieces[f"f{c}"] = (fwd, range(2 * n_rows + start, 2 * n_rows + start + blocks))
        start += blocks
    early = [pieces[p] for p in pieces if p not in LATE]
    late = [pieces[p] for p in LATE]
    late_slots = [at for _, slots in late for at in slots]

    gathered = lax.all_to_all(skel.reshape(devices, share, rank), AXES, 0, 0)
    gathered = gathered.reshape(width, rank)
    if share % 8 == 0:
        (expand,) = staged(
            functools.partial(tree_kernel, share),
            [gathered, coupling, transfer],
            [((width, rank), F32)],
            mib=TREE_MIB,
        )
    else:
        expand = tree_plain(gathered, transfer, coupling, share)
    expand = lax.all_to_all(expand.reshape(devices, share, rank), AXES, 0, 0)
    expand = expand.reshape(width, rank)

    total, left, far = staged(
        functools.partial(near_kernel, [slots for _, slots in early], late_slots),
        [order_perm, near_blocks, row_basis] + [rows for rows, _ in early],
        [((leaf, width), F32), ((2, leaf, len(late_slots) * BLK), BF16), ((2, leaf, rank), BF16)],
        smem=[band_offsets],
        scratch=[
            pltpu.VMEM((3 * n_rows, BLK, width), BF16),
            pltpu.VMEM((3 * n_rows, BLK, width), BF16),
            pltpu.VMEM((leaf, width), F32),
            pltpu.VMEM((len(late_slots) + 1, leaf, BLK), F32),
        ],
    )
    (product,) = staged(
        last_kernel,
        [expand, in_hbm(far), in_hbm(left), in_hbm(total)] + [rows for rows, _ in late],
        [((leaf, width), F32)],
        mib=LAST_MIB,
    )
    return product


def solution(mesh):
    split_rows = P(("gx", "gy"), None)
    placed = (split_rows,) * 4 + (P(("gx", "gy"), None, None, None), split_rows, P(), P())
    return jax.shard_map(body, mesh=mesh, in_specs=placed, out_specs=split_rows, check_vma=False)
```
